256 devices in a mesh: user: 16 (over z, core), item: 16 (over y, x).
Axes of the slice: x: 4, y: 4, z: 8, core: 2. Of those that a mesh axis runs over, the one named last changes fastest.
Arguments:
- confidence: bfloat16 [384, 16, 256, 256], P('user', 'item'), may hold values from 0 to 2
- tile_rows: int32 [384, 16], P('user', 'item'), may hold values from 0 to 3
- tile_cols: int32 [384, 16], P('user', 'item'), may hold values from 0 to 7, as said below
- tile_count: int32 [16, 16], P('user', 'item'), may hold values from 1 to 24, as said below
- item_factors: bfloat16 [16, 2048, 256], P('item', 'user'), may hold values from -2 to 2
Outputs:
- user_factors: float32 [16, 1024, 256], P('user', 'item')
The draws below stay inside these ranges and needn't reach their ends.
Inputs may be any that keep to these rules, and one draw needn't show every extreme that they name: `tile_cols`: item tile of a slot; the pairs (tile_rows, tile_cols) of one device's slots are distinct. `tile_count`: some device uses all 24 slots.
All inputs are finite; a program needn't handle non-finite values.
Results may differ from the reference program's by a relative error of at most 0.0045.
Values may be sent and summed in bfloat16 or wider, within the bound.
A program may use at most 64 MiB of HBM per device.

```python
import jax
import jax.numpy as jnp
from jax import lax

K = 256
TILE = 256
UTILES = 4
ITILES = 8
MAXT = 24
ITERS = 3
ITEMS = 32768
N_USER = 16
N_ITEM = 16


def slot_pattern(key):
    base_key = jax.random.fold_in(key, 11)
    key_list = jax.random.split(base_key, N_USER * N_ITEM)
    orders = jax.vmap(lambda single: jax.random.permutation(single, UTILES * ITILES))(key_list)
    picked = orders[:, :MAXT].astype(jnp.int32)
    picked = picked.reshape(N_USER, N_ITEM, MAXT).transpose(0, 2, 1)
    return picked.reshape(N_USER * MAXT, N_ITEM)


def draw_tile_rows(key, part):
    return slot_pattern(key) // ITILES


def draw_tile_cols(key, part):
    return slot_pattern(key) % ITILES


def draw_tile_count(key, part):
    divisor = jax.random.randint(jax.random.fold_in(key, 29), (N_USER * N_ITEM,), 1, 5)
    counts = (MAXT // divisor).astype(jnp.int32)
    chosen = jax.random.randint(jax.random.fold_in(key, 31), (), 0, N_USER * N_ITEM)
    counts = jnp.where(jnp.arange(N_USER * N_ITEM) == chosen, MAXT, counts).astype(jnp.int32)
    return counts.reshape(N_USER, N_ITEM)


def draw_item_factors(key, part):
    scale_key = jax.random.fold_in(key, 41)
    value_key = jax.random.fold_in(key, 43)
    block_key = jax.random.fold_in(key, 53)
    column_scale = jnp.exp(jax.random.uniform(scale_key, (K,), jnp.float32, jnp.log(0.3), jnp.log(3.0)))
    block_scale = jnp.exp(jax.random.uniform(block_key, (N_ITEM, ITILES, 1, 1), jnp.float32, jnp.log(0.2), jnp.log(5.0)))
    values = jnp.clip(jax.random.normal(value_key, (N_ITEM, ITILES * TILE, K), jnp.float32), -4.0, 4.0)
    values = (values.reshape(N_ITEM, ITILES, TILE, K) * block_scale).reshape(N_ITEM, ITILES * TILE, K)
    result = values * column_scale / jnp.sqrt(jnp.float32(ITEMS))
    return jnp.clip(result, -2.0, 2.0).astype(jnp.bfloat16)


def steps_of(rng, dims, cuts, low, largest):
    def one(dim, shards_of):
        heights = jax.random.uniform(jax.random.fold_in(jax.random.fold_in(rng, 6), dim), (shards_of,), jnp.float32, low / len(cuts), largest / len(cuts))
        return jnp.repeat(jnp.exp(heights), dims[dim] // shards_of).reshape((-1,) + (1,) * (len(dims) - dim - 1))

    loudness = one(*cuts[0])
    for cut in cuts[1:]:
        loudness = loudness * one(*cut)
    return loudness


def setup_inputs(seed: int = 0) -> dict:
    key_of = jax.random.split(jax.random.key(seed), 6)
    confidence = jnp.clip(2.0 * jax.random.uniform(key_of[0], (N_USER * MAXT, N_ITEM, TILE, TILE), jnp.float32) ** steps_of(key_of[0], (N_USER * MAXT, N_ITEM, TILE, TILE), ((0, 16), (1, 16)), -0.2, 0.2), 0.0, 2.0).astype(jnp.bfloat16)
    tile_rows = draw_tile_rows(jax.random.fold_in(key_of[5], 71), 0)
    tile_cols = draw_tile_cols(jax.random.fold_in(key_of[5], 71), 0)
    tile_count = draw_tile_count(jax.random.fold_in(key_of[5], 71), 0)
    item_factors = draw_item_factors(jax.random.fold_in(key_of[5], 71), 0)
    return {"confidence": confidence, "tile_rows": tile_rows, "tile_cols": tile_cols, "tile_count": tile_count, "item_factors": item_factors}


reg_weight = 0.1
tiny_eps = 1e-6


def device_tiles(conf_dev, rows_dev, cols_dev, count_dev, item_block):
    live_mask = (jnp.arange(conf_dev.shape[0]).astype(jnp.int32) < count_dev).astype(jnp.float32)
    y_blocks = item_block.reshape(ITILES, TILE, K)[cols_dev].astype(jnp.float32)
    weight_live = conf_dev.astype(jnp.float32) * live_mask[:, None, None]
    one_hot = (rows_dev[:, None] == jnp.arange(UTILES).astype(jnp.int32)[None, :]).astype(jnp.float32)
    return y_blocks, weight_live, one_hot, live_mask


def spread_rows(one_hot, contrib):
    placed = jnp.einsum("tu,tak->uak", one_hot, contrib, precision=lax.Precision.HIGHEST)
    return placed.reshape(UTILES * TILE, K)


def product_term(dirs_bf, conf_dev, rows_dev, cols_dev, count_dev, item_block):
    y_blocks, weight_live, one_hot, live_mask = device_tiles(conf_dev, rows_dev, cols_dev, count_dev, item_block)
    dir_blocks = dirs_bf.reshape(UTILES, TILE, K)[rows_dev].astype(jnp.float32)
    scores = jnp.einsum("tak,tbk->tab", dir_blocks, y_blocks, precision=lax.Precision.HIGHEST)
    weighted = lax.optimization_barrier((scores * weight_live).astype(jnp.bfloat16)).astype(jnp.float32)
    contrib = jnp.einsum("tab,tbk->tak", weighted, y_blocks, precision=lax.Precision.HIGHEST)
    return spread_rows(one_hot, contrib)


def rhs_term(dirs_bf, conf_dev, rows_dev, cols_dev, count_dev, item_block):
    y_blocks, weight_live, one_hot, live_mask = device_tiles(conf_dev, rows_dev, cols_dev, count_dev, item_block)
    contrib = jnp.einsum("tab,tbk->tak", weight_live, y_blocks, precision=lax.Precision.HIGHEST)
    contrib = contrib + live_mask[:, None, None] * jnp.sum(y_blocks, axis=1)[:, None, :]
    return spread_rows(one_hot, contrib)


def all_groups(term_fn, group_inputs, conf_all, rows_all, cols_all, count_all, item_factors):
    def one_group(operands):
        dirs_bf, conf_u, rows_u, cols_u, count_u = operands

        def add_device(total, pieces):
            conf_i, rows_i, cols_i, count_i, items_i = pieces
            return total + term_fn(dirs_bf, conf_i, rows_i, cols_i, count_i, items_i), None

        total, unused = lax.scan(add_device, jnp.zeros((UTILES * TILE, K), jnp.float32),
                                 (conf_u, rows_u, cols_u, count_u, item_factors))
        return total

    return lax.map(one_group, (group_inputs, conf_all, rows_all, cols_all, count_all))


def reference(confidence, tile_rows, tile_cols, tile_count, item_factors):
    conf_all = confidence.reshape(N_USER, MAXT, N_ITEM, TILE, TILE).transpose(0, 2, 1, 3, 4)
    rows_all = tile_rows.reshape(N_USER, MAXT, N_ITEM).transpose(0, 2, 1)
    cols_all = tile_cols.reshape(N_USER, MAXT, N_ITEM).transpose(0, 2, 1)
    flat_items = item_factors.reshape(-1, K).astype(jnp.float32)
    gram_matrix = jnp.dot(flat_items.T, flat_items, precision=lax.Precision.HIGHEST)
    placeholder = jnp.zeros((N_USER, UTILES * TILE, K), jnp.bfloat16)
    rhs_all = all_groups(rhs_term, placeholder, conf_all, rows_all, cols_all, tile_count, item_factors)
    solution = jnp.zeros_like(rhs_all)
    residual = rhs_all
    direction = rhs_all
    norm_now = jnp.sum(residual * residual, axis=-1, keepdims=True)
    for iteration in range(ITERS):
        tiles_part = all_groups(product_term, direction.astype(jnp.bfloat16), conf_all, rows_all, cols_all,
                                tile_count, item_factors)
        image = tiles_part + jnp.einsum("nuk,kj->nuj", direction, gram_matrix,
                                        precision=lax.Precision.HIGHEST) + reg_weight * direction
        alpha = norm_now / (jnp.sum(direction * image, axis=-1, keepdims=True) + tiny_eps)
        solution = solution + alpha * direction
        residual = residual - alpha * image
        if iteration + 1 < ITERS:
            norm_next = jnp.sum(residual * residual, axis=-1, keepdims=True)
            direction = residual + (norm_next / (norm_now + tiny_eps)) * direction
            norm_now = norm_next
    return solution
```

```python
import jax
import jax.numpy as jnp
from jax import lax
from jax.experimental import pallas as pl
from jax.experimental.pallas import tpu as pltpu
from jax.sharding import PartitionSpec as P

K = 256
TILE = 256
UTILES = 4
ITILES = 8
MAXT = 24
OWN = 64
SIDE = 4
PLANE = SIDE * SIDE
RING = 8
SHARD = 128
USERS = UTILES * TILE
ITEMS = ITILES * TILE
ROWS = K // PLANE

reg_weight = 0.1
tiny_eps = 1e-6

MESH = pl.DeviceIdType.MESH
F32 = jnp.float32
BF16 = jnp.bfloat16
HIGH = lax.Precision.HIGHEST


def blk(index, size):
    return pl.ds(pl.multiple_of(index * size, size), size)


def kernel(rows_ref, cols_ref, count_ref, conf_hbm, items_ref, out_ref,
           conf, yall, w, tbuf, dall, part, rbuf, qloc, qbuf,
           gfull, gpart, gown, gram, msum, colsum,
           sol, res, dirv, rr,
           keys, slots, lives,
           conf_sem, up_s, up_r, dn_s, dn_r, pa_s, pa_r,
           ag_s, ag_r, rs_s, rs_r, q_s, q_r, gp_s, gp_r, gz_s, gz_r):
    a = lax.axis_index("user")
    b = lax.axis_index("item")
    z, core = a // 2, a % 2
    y, x = b // SIDE, b % SIDE

    conf_copy = pltpu.make_async_copy(conf_hbm, conf, conf_sem)
    conf_copy.start()

    def plane(k):
        return ((y + k // SIDE) % SIDE) * SIDE + (x + k % SIDE) % SIDE

    def plane_from(k):
        return ((y + SIDE - k // SIDE) % SIDE) * SIDE + (x + SIDE - k % SIDE) % SIDE

    def group(j):
        return (a + j) % PLANE

    def group_from(j):
        return (a + PLANE - j) % PLANE

    def each(body):
        @pl.loop(1, PLANE)
        def _(k):
            body(k)

    def remote(src, dst, ssem, rsem, where):
        return pltpu.make_async_remote_copy(
            src_ref=src, dst_ref=dst, send_sem=ssem, recv_sem=rsem,
            device_id=where, device_id_type=MESH)

    barrier = pltpu.get_barrier_semaphore()

    def greet(k):
        pl.semaphore_signal(barrier, inc=1, device_id={"item": plane(k)}, device_id_type=MESH)
        pl.semaphore_signal(barrier, inc=1, device_id={"user": group(k)}, device_id_type=MESH)

    each(greet)

    for s in range(MAXT):
        live = s < count_ref[0, 0]
        keys[s] = jnp.where(live, rows_ref[s, 0] * ITILES + cols_ref[s, 0], -1)

    @pl.loop(0, UTILES * ITILES)
    def _(p):
        slot = jnp.int32(0)
        live = jnp.int32(0)
        for s in range(MAXT):
            hit = (keys[s] == p).astype(jnp.int32)
            slot = slot + s * hit
            live = live + hit
        slots[p] = slot
        lives[p] = live

    pl.semaphore_wait(barrier, 2 * (PLANE - 1))

    def shard(r, c):
        return ((z + r) % RING) * 2 + c

    def rows_of(r, c, first, size):
        return yall.at[pl.ds(pl.multiple_of(shard(r, c) * SHARD + first, 64), size)]

    def span(h, upward):
        if h < RING // 2:
            return 0, SHARD
        return (0, SHARD // 2) if upward else (SHARD // 2, SHARD // 2)

    def hop(h, upward, arriving):
        first, size = span(h, upward)
        r = (-1 if upward else 1) * (h if arriving else h - 1)
        r = (r + RING) % RING
        there = rows_of(r, core, first, size)
        src = there
        if h == 1 and not arriving:
            src = items_ref
        target = (z + (1 if upward else RING - 1)) % RING
        sems = (up_s, up_r) if upward else (dn_s, dn_r)
        return remote(src, there, sems[0].at[h], sems[1].at[h], {"user": target * 2 + core})

    def to_partner(r, arriving=False):
        there = rows_of(r, 1 - core if arriving else core, 0, SHARD)
        src = items_ref if (r == 0 and not arriving) else there
        return remote(src, there, pa_s.at[r], pa_r.at[r], {"user": z * 2 + 1 - core})

    hop(1, True, False).start()
    hop(1, False, False).start()
    to_partner(0).start()
    yall[blk(shard(0, core), SHARD), :] = items_ref[...]
    conf_copy.wait()

    def spread(u):
        @pl.loop(0, ITILES)
        def _(c):
            p = u * ITILES + c
            scale = lives[p].astype(F32).astype(BF16)
            w[u, :, blk(c, TILE)] = conf[slots[p]] * scale

    for h in range(1, RING // 2 + 1):
        spread(h - 1)
        hop(h, True, True).wait_recv()
        if h < RING // 2:
            hop(h + 1, True, False).start()
            to_partner(RING - h).start()
        hop(h, False, True).wait_recv()
        if h < RING // 2:
            hop(h + 1, False, False).start()
            to_partner(h).start()
        else:
            to_partner(RING // 2).start()
    for r in range(RING):
        to_partner(r, True).wait_recv()
    for h in range(1, RING // 2 + 1):
        hop(h, True, False).wait_send()
        hop(h, False, False).wait_send()
    for r in range(RING):
        to_partner(r).wait_send()

    for c in range(ITILES):
        colsum[c] = jnp.dot(jnp.ones((8, TILE), BF16), yall[c * TILE:(c + 1) * TILE, :],
                            preferred_element_type=F32)

    def own_rows(ref, who):
        return ref.at[blk(who, OWN)]

    def rs_send(k):
        return remote(own_rows(part, plane(k)), rbuf.at[k], rs_s.at[k], rs_r.at[k], {"item": plane(k)})

    def q_send(k):
        return remote(qloc.at[plane(k) // SIDE], qbuf.at[k], q_s.at[k], q_r.at[k], {"item": plane(k)})

    def ag_send(k):
        return remote(own_rows(dall, b), own_rows(dall, b), ag_s.at[k], ag_r.at[k], {"item": plane(k)})

    def ag_recv(k):
        who = plane_from(k)
        return remote(own_rows(dall, who), own_rows(dall, who), ag_s.at[k], ag_r.at[k], {"item": who})

    def gp_send(k):
        return remote(gfull.at[blk(a, ROWS)], gpart.at[k], gp_s.at[k], gp_r.at[k], {"item": plane(k)})

    def gz_send(j):
        return remote(gown, gram.at[blk(a, ROWS)], gz_s.at[j], gz_r.at[j], {"user": group(j)})

    def gz_recv(j):
        who = group_from(j)
        return remote(gown, gram.at[blk(who, ROWS)], gz_s.at[j], gz_r.at[j], {"user": who})

    def step_of(t):
        return (t * (t + 1) // 2) % SIDE

    def to_owners(t, send):
        for i in range(SIDE):
            k = step_of(t) * SIDE + i

            @pl.when(k != 0)
            def _():
                send(k).start()

    @pl.loop(0, UTILES)
    def _(t):
        u = (y + step_of(t)) % SIDE
        total = jnp.dot(w[u], yall[...], preferred_element_type=F32)
        base = jnp.zeros((8, K), F32)
        for c in range(ITILES):
            base = base + lives[u * ITILES + c].astype(F32) * colsum[c]
        msum[...] = base
        part[blk(u, TILE), :] = total + msum[0:1, :]
        to_owners(t, rs_send)

    gfull[...] = lax.dot_general(yall[...], yall[...], (((0,), (0,)), ((), ())), preferred_element_type=F32)
    each(lambda k: gp_send(k).start())

    def collect():
        res_own = part[blk(b, OWN), :]

        def add(k, total):
            rs_send(k).wait_recv()
            return total + rbuf[k]

        total = lax.fori_loop(1, PLANE, add, res_own)
        each(lambda k: rs_send(k).wait_send())
        return total

    def row_sum(v):
        return jnp.sum(v, axis=-1, keepdims=True)

    rhs = collect()
    sol[...] = jnp.zeros_like(sol)
    res[...] = rhs
    dirv[...] = rhs
    rr[...] = jnp.broadcast_to(row_sum(rhs * rhs), rr.shape)

    def share():
        dall[blk(b, OWN), :] = dirv[...].astype(BF16)
        each(lambda k: ag_send(k).start())

    def await_row(t):
        back = (SIDE - step_of(t)) % SIDE
        for i in range(SIDE):
            k = back * SIDE + i

            @pl.when(k != 0)
            def _():
                ag_recv(k).wait_recv()

    share()

    def add_gram(k, total):
        gp_send(k).wait_recv()
        return total + gpart[k]

    gown[...] = lax.fori_loop(1, PLANE, add_gram, gfull[blk(a, ROWS), :])
    each(lambda k: gz_send(k).start())
    gram[blk(a, ROWS), :] = gown[...]
    each(lambda k: gp_send(k).wait_send())

    def scores(u, c):
        return lax.dot_general(dall[blk(u, TILE), :], yall[c * TILE:(c + 1) * TILE, :],
                               (((1,), (1,)), ((), ())), preferred_element_type=F32)

    @pl.loop(0, 2)
    def _(it):
        @pl.loop(0, UTILES)
        def _(t):
            u = (y + step_of(t)) % SIDE
            await_row(t)
            for c in range(ITILES):
                cols = slice(c * TILE, (c + 1) * TILE)
                tbuf[:, cols] = (scores(u, c) * w[u, :, cols].astype(F32)).astype(BF16)
            part[blk(u, TILE), :] = jnp.dot(tbuf[...], yall[...], preferred_element_type=F32)
            to_owners(t, rs_send)

        @pl.when(it == 0)
        def _():
            each(lambda k: gz_recv(k).wait_recv())
            each(lambda k: gz_send(k).wait_send())

        d = dirv[...]
        dense = jnp.dot(d, gram[...], precision=HIGH, preferred_element_type=F32) + reg_weight * d
        each(lambda k: ag_send(k).wait_send())
        image = collect() + dense
        norm = rr[:, 0:1]
        alpha = norm / (row_sum(d * image) + tiny_eps)
        sol[...] = sol[...] + alpha * d
        left = res[...] - alpha * image
        res[...] = left
        new = row_sum(left * left)
        dirv[...] = left + new / (norm + tiny_eps) * d
        rr[...] = jnp.broadcast_to(new, rr.shape)
        share()

    ones = jnp.ones((8, 128), F32)

    @pl.loop(0, UTILES)
    def _(t):
        u = (y + step_of(t)) % SIDE
        await_row(t)
        lanes = jnp.zeros((TILE, 128), F32)
        for c in range(ITILES):
            cols = slice(c * TILE, (c + 1) * TILE)
            s = scores(u, c)
            prod = (s * w[u, :, cols].astype(F32)).astype(BF16).astype(F32) * s
            lanes = lanes + prod[:, :128] + prod[:, 128:]
        qloc[u] = lax.dot_general(ones, lanes, (((1,), (1,)), ((), ())), precision=HIGH,
                                  preferred_element_type=F32)
        to_owners(t, q_send)

    d = dirv[...]
    dense = jnp.dot(d, gram[...], precision=HIGH, preferred_element_type=F32) + reg_weight * d
    own = row_sum(d * dense)
    each(lambda k: ag_send(k).wait_send())

    def add_q(k, total):
        q_send(k).wait_recv()
        return total + qbuf[k]

    q = lax.fori_loop(1, PLANE, add_q, qloc[y])
    each(lambda k: q_send(k).wait_send())
    msum[...] = q
    wide = jnp.broadcast_to(msum[0:1, :], (OWN, TILE))
    lane = lax.broadcasted_iota(jnp.int32, (OWN, TILE), 1)
    row = lax.broadcasted_iota(jnp.int32, (OWN, TILE), 0)
    tiles = row_sum(jnp.where(lane == row + x * OWN, wide, 0.0))
    alpha = rr[:, 0:1] / (tiles + own + tiny_eps)
    out_ref[...] = sol[...] + alpha * d


def shards(confidence, tile_rows, tile_cols, tile_count, item_factors):
    vmem = pl.BlockSpec(memory_space=pltpu.VMEM)
    smem = pl.BlockSpec(memory_space=pltpu.SMEM)
    dma = pltpu.SemaphoreType.DMA
    out = pl.pallas_call(
        kernel,
        out_shape=jax.ShapeDtypeStruct((OWN, K), F32),
        in_specs=[smem, smem, smem, pl.BlockSpec(memory_space=pl.ANY), vmem],
        out_specs=vmem,
        scratch_shapes=[
            pltpu.VMEM((MAXT, TILE, TILE), BF16),
            pltpu.VMEM((ITEMS, K), BF16),
            pltpu.VMEM((UTILES, TILE, ITEMS), BF16),
            pltpu.VMEM((TILE, ITEMS), BF16),
            pltpu.VMEM((USERS, K), BF16),
            pltpu.VMEM((USERS, K), F32),
            pltpu.VMEM((PLANE, OWN, K), F32),
            pltpu.VMEM((UTILES, 8, TILE), F32),
            pltpu.VMEM((PLANE, 8, TILE), F32),
            pltpu.VMEM((K, K), F32),
            pltpu.VMEM((PLANE, ROWS, K), F32),
            pltpu.VMEM((ROWS, K), F32),
            pltpu.VMEM((K, K), F32),
            pltpu.VMEM((8, K), F32),
            pltpu.VMEM((ITILES, 8, K), F32),
            pltpu.VMEM((OWN, K), F32),
            pltpu.VMEM((OWN, K), F32),
            pltpu.VMEM((OWN, K), F32),
            pltpu.VMEM((OWN, 128), F32),
            pltpu.SMEM((MAXT,), jnp.int32),
            pltpu.SMEM((UTILES * ITILES,), jnp.int32),
            pltpu.SMEM((UTILES * ITILES,), jnp.int32),
            dma,
            dma((5,)), dma((5,)), dma((5,)), dma((5,)), dma((RING,)), dma((RING,)),
        ] + [dma((PLANE,))] * 10,
        compiler_params=pltpu.CompilerParams(
            collective_id=0, has_side_effects=True, vmem_limit_bytes=60 * 1024 * 1024),
    )(tile_rows, tile_cols, tile_count, confidence.reshape(MAXT, TILE, TILE), item_factors[0])
    return out[None]


def solution(mesh):
    in_specs = (
        P("user", "item", None, None),
        P("user", "item"),
        P("user", "item"),
        P("user", "item"),
        P("item", "user", None),
    )
    out_specs = P("user", "item", None)
    return jax.shard_map(shards, mesh=mesh, in_specs=in_specs, out_specs=out_specs, check_vma=False)
```
